256 devices in a mesh: blk: 128 (over z, y_lo, x, core), dp: 2 (over y_hi).
Axes of the slice: x: 4, y: 4 (y_hi: 2, y_lo: 2; y = y_hi * 2 + y_lo), z: 8, core: 2. Of those that a mesh axis runs over, the one named last changes fastest.
Arguments:
- tokens: bfloat16 [49152, 2048], P(('blk', 'dp')), may hold values from -6 to 6
- cotangent: bfloat16 [49152, 2048], P(('blk', 'dp')), may hold values from -0.59765625 to 0.59765625
- gate_probs: bfloat16 [49152, 3], P(('blk', 'dp')), may hold values from 0.099609375 to 1
- slot_rows: int32 [384, 128], P('blk'), may hold values from 0 to 384, as said below
- w_gate: bfloat16 [128, 2048, 768], P('blk', None, 'dp'), may hold values from -0.125 to 0.125
- w_up: bfloat16 [128, 2048, 768], P('blk', None, 'dp'), may hold values from -0.125 to 0.125
- w_down: bfloat16 [128, 768, 2048], P('blk', 'dp'), may hold values from -0.21875 to 0.21875
Outputs:
- mixed: bfloat16 [49152, 2048], P(('blk', 'dp'))
- input_grad: bfloat16 [49152, 2048], P(('blk', 'dp'))
- gate_grad: float32 [49152, 3], P(('blk', 'dp'))
- w_gate_grad: bfloat16 [128, 2048, 768], P('blk', None, 'dp')
- w_up_grad: bfloat16 [128, 2048, 768], P('blk', None, 'dp')
- w_down_grad: bfloat16 [128, 768, 2048], P('blk', 'dp')
The draws below stay inside these ranges and needn't reach their ends.
Inputs may be any that keep to these rules, and one draw needn't show every extreme that they name: `slot_rows`: entries below 384 in a row are distinct and stand before the entries equal to 384; every row names at least 16 tokens, and some row names 128.
All inputs are finite; a program needn't handle non-finite values.
Results may differ from the reference program's by a relative error of at most 0.0075.
Values may be sent and summed in bfloat16 or wider, within the bound.
A program may use at most 128 MiB of HBM per device.

```python
import jax
import jax.numpy as jnp
from jax import lax

D = 2048
H = 768
CYCLE = 3
CAP = 128
GROUP = 384
EXPERTS = 128
TOKENS = 49152
LISTS = 384
N_BLK = 128


def draw_slot_rows(key, part):
    side_key, full_key, perm_key = jax.random.split(key, 3)
    side_length = jax.random.randint(side_key, (LISTS,), 4, 12)
    counts = side_length * side_length * CAP // 128
    full_index = jax.random.randint(full_key, (), 0, LISTS)
    counts = jnp.where(jnp.arange(LISTS) == full_index, CAP, counts)
    list_keys = jax.random.split(perm_key, LISTS)
    shuffled = jax.vmap(lambda list_key: jax.random.permutation(list_key, GROUP)[:CAP])(list_keys)
    slot_index = jnp.arange(CAP)[None, :]
    return jnp.where(slot_index < counts[:, None], shuffled, GROUP).astype(jnp.int32)


def level_of(key, shape, cuts, least, largest):
    factor_of, own = 1.0, jax.random.fold_in(key, 6)
    for dim, blocks in cuts:
        draws = jnp.exp(jax.random.uniform(jax.random.fold_in(own, dim), (blocks,), jnp.float32, least / len(cuts), largest / len(cuts)))
        factor_of = factor_of * jnp.repeat(draws, shape[dim] // blocks).reshape([-1 if axis == dim else 1 for axis in range(len(shape))])
    return factor_of


def gaussian(stream_key, shape, width, most, pieces=(), kind=jnp.bfloat16):
    gain = level_of(stream_key, shape, pieces, -0.22, 0.18) if pieces else 1.0
    drawn = jax.random.normal(stream_key, shape, jnp.float32) * width * gain
    return jnp.minimum(jnp.maximum(drawn, -most), most).astype(kind)


def setup_inputs(seed: int = 0) -> dict:
    key_of = jax.random.split(jax.random.key(seed), 8)
    tokens = gaussian(key_of[0], (TOKENS, D), 1.0, 6.0, ((0, 256),))
    cotangent = gaussian(key_of[1], (TOKENS, D), 0.1, 0.59765625, ((0, 256),))
    gate_probs = jnp.clip(0.099609375 + 0.9003906 * jax.random.uniform(key_of[2], (TOKENS, CYCLE), jnp.float32) ** level_of(key_of[2], (TOKENS, CYCLE), ((0, 256),), -0.2, 0.2), 0.099609375, 1.0).astype(jnp.bfloat16)
    slot_rows = draw_slot_rows(jax.random.fold_in(key_of[7], 71), 0)
    w_gate = gaussian(key_of[4], (EXPERTS, D, H), D ** -0.5, 0.125, ((0, 128), (2, 2)))
    w_up = gaussian(key_of[5], (EXPERTS, D, H), D ** -0.5, 0.125, ((0, 128), (2, 2)))
    w_down = gaussian(key_of[6], (EXPERTS, H, D), H ** -0.5, 0.21875, ((0, 128), (1, 2)))
    return {"tokens": tokens, "cotangent": cotangent, "gate_probs": gate_probs, "slot_rows": slot_rows, "w_gate": w_gate, "w_up": w_up, "w_down": w_down}


def expert_step(slab, rows_x, rows_dy, rows_gate):
    w_gate_s, w_up_s, w_down_s = slab
    gate_rows = rows_gate.astype(jnp.float32)
    pre_gate = jnp.dot(rows_x, w_gate_s, preferred_element_type=jnp.float32)
    pre_up = jnp.dot(rows_x, w_up_s, preferred_element_type=jnp.float32)
    sigmoid_gate = jax.nn.sigmoid(pre_gate)
    active = pre_gate * sigmoid_gate
    hidden = (active * pre_up).astype(jnp.bfloat16)
    expert_out = jnp.dot(hidden, w_down_s, preferred_element_type=jnp.float32)
    weighted = gate_rows[:, None] * expert_out
    cotan_rows = rows_dy.astype(jnp.float32)
    gate_grad = jnp.sum(cotan_rows * expert_out, axis=1)
    out_grad = (gate_rows[:, None] * cotan_rows).astype(jnp.bfloat16)
    hidden_grad = jnp.einsum("cd,hd->ch", out_grad, w_down_s, preferred_element_type=jnp.float32)
    pre_gate_grad = (hidden_grad * pre_up * sigmoid_gate * (1.0 + pre_gate * (1.0 - sigmoid_gate))).astype(jnp.bfloat16)
    pre_up_grad = (hidden_grad * active).astype(jnp.bfloat16)
    input_grad = jnp.einsum("ch,dh->cd", pre_gate_grad, w_gate_s, preferred_element_type=jnp.float32)
    input_grad = input_grad + jnp.einsum("ch,dh->cd", pre_up_grad, w_up_s, preferred_element_type=jnp.float32)
    part_gate = jnp.einsum("cd,ch->dh", rows_x, pre_gate_grad, preferred_element_type=jnp.float32).astype(jnp.bfloat16)
    part_up = jnp.einsum("cd,ch->dh", rows_x, pre_up_grad, preferred_element_type=jnp.float32).astype(jnp.bfloat16)
    part_down = jnp.einsum("ch,cd->hd", hidden, out_grad, preferred_element_type=jnp.float32).astype(jnp.bfloat16)
    return (weighted, input_grad, gate_grad), (part_gate, part_up, part_down)


def reference(tokens, cotangent, gate_probs, slot_rows, w_gate, w_up, w_down):
    padded_x = jnp.concatenate([tokens.reshape(N_BLK, GROUP, D), jnp.zeros((N_BLK, 1, D), tokens.dtype)], axis=1)
    padded_dy = jnp.concatenate([cotangent.reshape(N_BLK, GROUP, D), jnp.zeros((N_BLK, 1, D), cotangent.dtype)], axis=1)
    padded_gate = jnp.concatenate([gate_probs.reshape(N_BLK, GROUP, CYCLE), jnp.zeros((N_BLK, 1, CYCLE), gate_probs.dtype)], axis=1)
    all_lists = slot_rows.reshape(N_BLK, CYCLE, CAP)

    def expert_block(expert_index):
        slab = (w_gate[expert_index], w_up[expert_index], w_down[expert_index])
        weighted_list = []
        input_list = []
        gate_list = []
        totals = None
        for cycle_step in range(CYCLE):
            group_index = ((expert_index + cycle_step) % N_BLK).astype(jnp.int32)
            list_rows = all_lists[group_index, cycle_step]
            rows_x = padded_x[group_index][list_rows]
            rows_dy = padded_dy[group_index][list_rows]
            rows_gate = padded_gate[group_index][list_rows, cycle_step]
            results, partials = expert_step(slab, rows_x, rows_dy, rows_gate)
            weighted_list.append(results[0])
            input_list.append(results[1])
            gate_list.append(results[2])
            widened = tuple(piece.astype(jnp.float32) for piece in partials)
            if totals is None:
                totals = widened
            else:
                totals = tuple(first + second for first, second in zip(totals, widened))
        grads = tuple(piece.astype(jnp.bfloat16) for piece in totals)
        return jnp.stack(weighted_list), jnp.stack(input_list), jnp.stack(gate_list), grads

    weighted_all, input_all, gate_all, grads = lax.map(expert_block, jnp.arange(N_BLK, dtype=jnp.int32))

    mixed_acc = jnp.zeros((N_BLK, GROUP + 1, D), jnp.float32)
    input_acc = jnp.zeros((N_BLK, GROUP + 1, D), jnp.float32)
    gate_acc = jnp.zeros((N_BLK, GROUP + 1, CYCLE), jnp.float32)
    for cycle_step in range(CYCLE):
        step_rows = all_lists[:, cycle_step]
        step_weighted = jnp.roll(weighted_all[:, cycle_step], cycle_step, axis=0)
        step_input = jnp.roll(input_all[:, cycle_step], cycle_step, axis=0)
        step_gate = jnp.roll(gate_all[:, cycle_step], cycle_step, axis=0)
        mixed_acc = jax.vmap(lambda accum, where, values: accum.at[where].add(values))(mixed_acc, step_rows, step_weighted)
        input_acc = jax.vmap(lambda accum, where, values: accum.at[where].add(values))(input_acc, step_rows, step_input)
        gate_acc = jax.vmap(lambda accum, where, values: accum.at[where, cycle_step].add(values))(gate_acc, step_rows, step_gate)
    mixed = mixed_acc[:, :GROUP].reshape(TOKENS, D).astype(jnp.bfloat16)
    input_grad = input_acc[:, :GROUP].reshape(TOKENS, D).astype(jnp.bfloat16)
    gate_grad = gate_acc[:, :GROUP].reshape(TOKENS, CYCLE)
    return mixed, input_grad, gate_grad, grads[0], grads[1], grads[2]
```

```python
import jax
import jax.numpy as jnp
from jax import lax
from jax.sharding import PartitionSpec as P

BF = jnp.bfloat16
F32 = jnp.float32


def shifted(value, axis, steps):
    count = lax.axis_size(axis)
    pairs = [(source, (source + steps) % count) for source in range(count)]
    return lax.ppermute(value, axis, pairs)


def on_device(tokens, cotangent, gate_probs, slot_rows, w_gate, w_up, w_down):
    half = lax.axis_index("dp")
    own = tokens.shape[0]
    group_x = lax.all_gather(tokens, "dp", axis=0, tiled=True)
    group_dy = lax.all_gather(cotangent, "dp", axis=0, tiled=True)
    group_gate = lax.all_gather(gate_probs, "dp", axis=0, tiled=True)
    cycle, cap = slot_rows.shape
    group = group_x.shape[0]
    names = slot_rows[:, :, None] == lax.broadcasted_iota(jnp.int32, (1, 1, group), 2)
    picks = names.astype(BF)
    rows_x = jnp.einsum("sct,td->scd", picks, group_x, preferred_element_type=F32).astype(BF)
    rows_dy = jnp.einsum("sct,td->scd", picks, group_dy, preferred_element_type=F32).astype(BF)
    rows_gate = jnp.einsum("sct,ts->sc", picks, group_gate, preferred_element_type=F32).astype(BF)
    lists_x, lists_dy, lists_gate = [rows_x[0]], [rows_dy[0]], [rows_gate[0]]
    for step in range(1, cycle):
        lists_x.append(shifted(rows_x[step], "blk", -step))
        lists_dy.append(shifted(rows_dy[step], "blk", -step))
        lists_gate.append(shifted(rows_gate[step], "blk", -step))
    x = jnp.concatenate(lists_x, axis=0)
    dy = jnp.concatenate(lists_dy, axis=0)
    gate = jnp.concatenate(lists_gate, axis=0).astype(F32)[:, None]
    w_g, w_u, w_d = w_gate[0], w_up[0], w_down[0]
    pre_gate = jnp.dot(x, w_g, preferred_element_type=F32)
    pre_up = jnp.dot(x, w_u, preferred_element_type=F32)
    back = jnp.einsum("cd,hd->ch", dy, w_d, preferred_element_type=F32)
    sig = jax.nn.sigmoid(pre_gate)
    active = pre_gate * sig
    hidden = active * pre_up
    gate_part = jnp.sum(hidden * back, axis=1)
    hidden_w = (hidden * gate).astype(BF)
    hidden_grad = back * gate
    pgg = (hidden_grad * pre_up * sig * (1.0 + pre_gate * (1.0 - sig))).astype(BF)
    pug = (hidden_grad * active).astype(BF)
    weighted = jnp.dot(hidden_w, w_d, preferred_element_type=F32).astype(BF)
    in_grad = jnp.einsum("ch,dh->cd", pgg, w_g, preferred_element_type=F32)
    in_grad = in_grad + jnp.einsum("ch,dh->cd", pug, w_u, preferred_element_type=F32)
    in_grad = in_grad.astype(BF)
    out_w, out_i, out_g = [weighted[:cap]], [in_grad[:cap]], [gate_part[:cap]]
    for step in range(1, cycle):
        rows = slice(step * cap, (step + 1) * cap)
        out_w.append(shifted(weighted[rows], "blk", step))
        out_i.append(shifted(in_grad[rows], "blk", step))
        out_g.append(shifted(gate_part[rows], "blk", step))
    d_gate = jnp.einsum("cd,ch->dh", x, pgg, preferred_element_type=F32).astype(BF)
    d_up = jnp.einsum("cd,ch->dh", x, pug, preferred_element_type=F32).astype(BF)
    d_down = jnp.einsum("ch,cd->hd", hidden_w, dy, preferred_element_type=F32).astype(BF)
    back_w = jnp.concatenate(out_w, axis=0)
    back_i = jnp.concatenate(out_i, axis=0)
    flat = picks.reshape(cycle * cap, group)
    mixed = jnp.einsum("ct,cd->td", flat, back_w, preferred_element_type=F32)
    input_grad = jnp.einsum("ct,cd->td", flat, back_i, preferred_element_type=F32)
    gate_grad = jnp.stack(
        [jnp.sum(jnp.where(names[s], out_g[s][:, None], 0.0), axis=0) for s in range(cycle)], axis=1
    )

    def summed(full, kind):
        mine = lax.dynamic_slice_in_dim(full, half * own, own, 0)
        other = lax.dynamic_slice_in_dim(full, (1 - half) * own, own, 0)
        arrived = lax.ppermute(other.astype(kind), "dp", [(0, 1), (1, 0)])
        return mine + arrived.astype(F32)

    return (
        summed(mixed, BF).astype(BF),
        summed(input_grad, BF).astype(BF),
        summed(gate_grad, F32),
        d_gate[None],
        d_up[None],
        d_down[None],
    )


def solution(mesh):
    in_specs = (
        P(("blk", "dp"), None),
        P(("blk", "dp"), None),
        P(("blk", "dp"), None),
        P("blk", None),
        P("blk", None, "dp"),
        P("blk", None, "dp"),
        P("blk", "dp", None),
    )
    out_specs = (
        P(("blk", "dp"), None),
        P(("blk", "dp"), None),
        P(("blk", "dp"), None),
        P("blk", None, "dp"),
        P("blk", None, "dp"),
        P("blk", "dp", None),
    )
    return jax.shard_map(
        on_device, mesh=mesh, in_specs=in_specs, out_specs=out_specs, check_vma=False
    )
```

```python
import jax
import jax.numpy as jnp
from jax import lax
from jax.experimental import pallas as pl
from jax.experimental.pallas import tpu as pltpu
from jax.sharding import PartitionSpec as P

BF = jnp.bfloat16
F32 = jnp.float32
MESH = pl.DeviceIdType.MESH
CHUNKS = 8


def dot(a, b, ca=1, cb=0):
    return lax.dot_general(a, b, (((ca,), (cb,)), ((), ())), preferred_element_type=F32)


def kernel(
    blocks, tok, cot, gate, slots, w_g, w_u, w_d,
    o_mix, o_in, o_gate, o_dg, o_du, o_dd,
    X, E, S, G, EG, GS, WGU, WD, PICK, PUT, PRE, BACK, PGU, HW, R, RR, GG, GGS, OWN, YS, YR, OUT, DGU, DD,
    ld_x, ld_w, ld_d, ld_g, yf_s, yf_r, yg_s, yg_r, xf_s, xf_r, xg_s, xg_r, xr_s, xr_r, gg_s, gg_r, yr_s, yr_r,
    st_o, st_w, st_d,
):
    nc, _, _, cw = X.shape
    own, cap = tok.shape[0], slots.shape[1]
    hid = WD.shape[1]
    b, h = lax.axis_index("blk"), lax.axis_index("dp")
    peer = (b, 1 - h)
    x8 = lax.rem(b, 8)

    def down(s):
        return lax.rem(b + blocks - s, blocks)

    def up(s):
        return lax.rem(b + s, blocks)

    def down_dev(s, c):
        cross = 1 - lax.div(x8 + 8 - s, 8)
        return (down(s), lax.rem(h + cross * lax.rem(c, 2), 2))

    def up_dev(s, c):
        cross = lax.div(x8 + s, 8)
        return (up(s), lax.rem(h + cross * lax.rem(c, 2), 2))

    def cols(c):
        return pl.ds(pl.multiple_of(c * cw, cw), cw)

    def load_x(k, c):
        return pltpu.make_async_copy((tok, cot)[k].at[:, cols(c)], X.at[c, k, pl.ds(0, own)], ld_x.at[k, c])

    def send_y(k, c):
        return pltpu.make_async_remote_copy(
            (tok, cot)[k].at[:, cols(c)], X.at[c, k, pl.ds(own, own)], yf_s.at[k, c], yf_r.at[k, c],
            device_id=peer, device_id_type=MESH)

    def send_x(s, c):
        return pltpu.make_async_remote_copy(
            S.at[c, s - 1], E.at[c, s], xf_s.at[s - 1, c], xf_r.at[s - 1, c],
            device_id=down_dev(s, c), device_id_type=MESH)

    def send_back(s, c):
        return pltpu.make_async_remote_copy(
            R.at[c, s - 1], RR.at[c, s], xr_s.at[s - 1, c], xr_r.at[s - 1, c],
            device_id=up_dev(s, c), device_id_type=MESH)

    def send_sum(c):
        return pltpu.make_async_remote_copy(
            YS.at[c], YR.at[c], yr_s.at[c], yr_r.at[c], device_id=peer, device_id_type=MESH)

    def send_gate():
        return pltpu.make_async_remote_copy(
            gate, G.at[pl.ds(own, own)], yg_s, yg_r, device_id=peer, device_id_type=MESH)

    def send_list_gate(s):
        return pltpu.make_async_remote_copy(
            GS.at[s - 1], EG.at[s], xg_s.at[s - 1], xg_r.at[s - 1],
            device_id=(down(s), h), device_id_type=MESH)

    def send_gate_grad(s, rel):
        source = GG.at[0, 0] if s == 0 else GGS.at[s - 1]
        target = (up(s), h if rel == 0 else 1 - h)
        return pltpu.make_async_remote_copy(
            source, GG.at[s, rel], gg_s.at[s, rel], gg_r.at[s, rel], device_id=target, device_id_type=MESH)

    routes = [(0, 1), (1, 0), (1, 1), (2, 0), (2, 1)]

    bar = pltpu.get_barrier_semaphore()
    near = [peer] + [(f(s), d) for f in (down, up) for s in (1, 2) for d in (h, 1 - h)]
    for device in near:
        pl.semaphore_signal(bar, inc=1, device_id=device, device_id_type=MESH)
    load_gate = pltpu.make_async_copy(gate, G.at[pl.ds(0, own)], ld_g)
    load_gate.start()

    def begin(c, _):
        load_x(0, c).start()
        load_x(1, c).start()
        return 0

    lax.fori_loop(0, nc, begin, 0)
    pl.semaphore_wait(bar, len(near))
    send_gate().start()

    def cross(c, _):
        send_y(0, c).start()
        send_y(1, c).start()
        return 0

    lax.fori_loop(0, nc, cross, 0)
    load_wg = pltpu.make_async_copy(w_g.at[0], WGU.at[:, pl.ds(0, hid)], ld_w.at[0])
    load_wu = pltpu.make_async_copy(w_u.at[0], WGU.at[:, pl.ds(hid, hid)], ld_w.at[1])
    load_wg.start()
    load_wu.start()

    def load_wd(c):
        return pltpu.make_async_copy(w_d.at[0, :, cols(c)], WD.at[c], ld_d.at[c])

    def begin_d(c, _):
        load_wd(c).start()
        return 0

    lax.fori_loop(0, nc, begin_d, 0)

    for s in range(3):
        row = slots[s : s + 1, :]
        at = lax.broadcasted_iota(jnp.int32, (own, cap), 0)
        mine = jnp.where(row == at + h * own, 1.0, 0.0).astype(F32)
        other = jnp.where(row == at + (1 - h) * own, 1.0, 0.0).astype(F32)
        PUT[0:own, s * cap : (s + 1) * cap] = mine.astype(BF)
        PUT[own : 2 * own, s * cap : (s + 1) * cap] = other.astype(BF)
        both = jnp.concatenate([mine, other], axis=0)
        PICK[s * cap : (s + 1) * cap, :] = both.T.astype(BF)
    PRE[...] = jnp.zeros_like(PRE)
    BACK[...] = jnp.zeros_like(BACK)

    load_gate.wait()
    send_gate().wait_recv()
    for s in (2, 1, 0):
        picked = dot(PICK[s * cap : (s + 1) * cap, :], G[...]).astype(BF)
        if s:
            GS[s - 1] = picked
            send_list_gate(s).start()
        else:
            EG[0] = picked
    load_wg.wait()
    load_wu.wait()

    def project(c):
        send_x(1, c).wait_recv()
        send_x(2, c).wait_recv()
        load_wd(c).wait()
        x = E[c, :, 0].reshape(3 * cap, cw)
        dy = E[c, :, 1].reshape(3 * cap, cw)
        PRE[...] += dot(x, WGU[pl.ds(pl.multiple_of(c * cw, cw), cw), :])
        BACK[...] += dot(dy, WD[c], 1, 1)

    def forward(c, _):
        for k in range(2):
            load_x(k, c).wait()
            send_y(k, c).wait_recv()
        for k in range(2):
            rows = dot(PICK[...], X[c, k]).astype(BF)
            E[c, 0, k] = rows[0:cap]
            S[c, 0, k] = rows[cap : 2 * cap]
            S[c, 1, k] = rows[2 * cap : 3 * cap]
        send_x(2, c).start()
        send_x(1, c).start()

        @pl.when(c > 0)
        def _():
            project(c - 1)

        return 0

    lax.fori_loop(0, nc, forward, 0)
    project(nc - 1)
    send_list_gate(1).wait_recv()
    send_list_gate(2).wait_recv()

    for s in range(3):
        rows = slice(s * cap, (s + 1) * cap)
        gate_col = EG[s].astype(F32)[:, s : s + 1]
        pre_gate = PRE[rows, 0:hid]
        pre_up = PRE[rows, hid : 2 * hid]
        back = BACK[rows, :]
        sig = jax.nn.sigmoid(pre_gate)
        active = pre_gate * sig
        hidden = active * pre_up
        part = jnp.sum(hidden * back, axis=1, keepdims=True)
        part = jnp.broadcast_to(part, (cap, cap)).T[0:8, :]
        if s == 0:
            GG[0, 0] = part
        else:
            GGS[s - 1] = part
        grad = back * gate_col
        HW[rows, :] = (hidden * gate_col).astype(BF)
        PGU[rows, 0:hid] = (grad * pre_up * sig * (1.0 + pre_gate * (1.0 - sig))).astype(BF)
        PGU[rows, hid : 2 * hid] = (grad * active).astype(BF)

    def results(c, _):
        weighted = dot(HW[...], WD[c]).astype(BF)
        in_grad = dot(PGU[...], WGU[pl.ds(pl.multiple_of(c * cw, cw), cw), :], 1, 1).astype(BF)
        for k, value in enumerate((weighted, in_grad)):
            RR[c, 0, k] = value[0:cap]
            R[c, 0, k] = value[cap : 2 * cap]
            R[c, 1, k] = value[2 * cap : 3 * cap]
        send_back(2, c).start()
        send_back(1, c).start()
        return 0

    lax.fori_loop(0, nc, results, 0)
    for s, rel in routes:
        send_gate_grad(s, rel).start()

    def store_w(k, c):
        target = (o_dg, o_du)[k].at[0, pl.ds(pl.multiple_of(c * cw, cw), cw), :]
        return pltpu.make_async_copy(DGU.at[c, :, pl.ds(k * hid, hid)], target, st_w.at[k, c])

    def store_d(c):
        return pltpu.make_async_copy(DD.at[c], o_dd.at[0, :, cols(c)], st_d.at[c])

    def weight_grads(c, _):
        x = E[c, :, 0].reshape(3 * cap, cw)
        dy = E[c, :, 1].reshape(3 * cap, cw)
        DGU[c] = dot(x, PGU[...], 0, 0).astype(BF)
        DD[c] = dot(HW[...], dy, 0, 0).astype(BF)
        store_w(0, c).start()
        store_w(1, c).start()
        store_d(c).start()
        return 0

    lax.fori_loop(0, nc, weight_grads, 0)

    def store_out(k, c):
        return pltpu.make_async_copy(OUT.at[c, k], (o_mix, o_in)[k].at[:, cols(c)], st_o.at[k, c])

    def finish(c):
        send_sum(c).wait_recv()
        for k in range(2):
            OUT[c, k] = (OWN[c, k] + YR[c, k].astype(F32)).astype(BF)
            store_out(k, c).start()

    def collect(c, _):
        send_back(1, c).wait_recv()
        send_back(2, c).wait_recv()
        for k in range(2):
            rows = RR[c, :, k].reshape(3 * cap, cw)
            total = dot(PUT[...], rows)
            YS[c, k] = total[own : 2 * own].astype(BF)
            OWN[c, k] = total[0:own]
        send_sum(c).start()

        @pl.when(c > 1)
        def _():
            finish(c - 2)

        return 0

    lax.fori_loop(0, nc, collect, 0)

    for s, rel in routes:
        send_gate_grad(s, rel).wait_recv()
    lane = lax.broadcasted_iota(jnp.int32, (own, cap), 1)
    grads = jnp.zeros((own, cap), F32)
    for s in range(3):
        row = GG[s, 0][0:1, :] + GG[s, 1][0:1, :]
        named = PUT[0:own, s * cap : (s + 1) * cap].astype(F32)
        column = jnp.sum(jnp.where(named > 0.5, jnp.broadcast_to(row, (own, cap)), 0.0), axis=1, keepdims=True)
        grads = jnp.where(lane == s, column, grads)
    o_gate[...] = grads

    finish(nc - 2)
    finish(nc - 1)

    send_gate().wait_send()
    for s in (1, 2):
        send_list_gate(s).wait_send()
    for s, rel in routes:
        send_gate_grad(s, rel).wait_send()

    def drain(c, _):
        for k in range(2):
            send_y(k, c).wait_send()
            store_w(k, c).wait()
            store_out(k, c).wait()
        for s in (1, 2):
            send_x(s, c).wait_send()
            send_back(s, c).wait_send()
        send_sum(c).wait_send()
        store_d(c).wait()
        return 0

    lax.fori_loop(0, nc, drain, 0)


def on_device(tokens, cotangent, gate_probs, slot_rows, w_gate, w_up, w_down):
    own, width = tokens.shape
    cycle, cap = slot_rows.shape
    hid = w_gate.shape[2]
    nc, cw = CHUNKS, width // CHUNKS
    group, lists = 2 * own, cycle * cap
    blocks = lax.axis_size("blk")
    padded = jnp.pad(gate_probs, ((0, 0), (0, cap - cycle)))
    dma = pltpu.SemaphoreType.DMA
    vmem = pltpu.VMEM
    any_space = pl.BlockSpec(memory_space=pl.ANY)
    in_vmem = pl.BlockSpec(memory_space=pltpu.VMEM)

    def body(*refs):
        kernel(blocks, *refs)

    outs = pl.pallas_call(
        body,
        out_shape=(
            jax.ShapeDtypeStruct((own, width), BF),
            jax.ShapeDtypeStruct((own, width), BF),
            jax.ShapeDtypeStruct((own, cap), F32),
            jax.ShapeDtypeStruct(w_gate.shape, BF),
            jax.ShapeDtypeStruct(w_up.shape, BF),
            jax.ShapeDtypeStruct(w_down.shape, BF),
        ),
        in_specs=[any_space, any_space, any_space, in_vmem, any_space, any_space, any_space],
        out_specs=(any_space, any_space, in_vmem, any_space, any_space, any_space),
        scratch_shapes=[
            vmem((nc, 2, group, cw), BF),
            vmem((nc, cycle, 2, cap, cw), BF),
            vmem((nc, cycle - 1, 2, cap, cw), BF),
            vmem((group, cap), BF),
            vmem((cycle, cap, cap), BF),
            vmem((cycle - 1, cap, cap), BF),
            vmem((width, 2 * hid), BF),
            vmem((nc, hid, cw), BF),
            vmem((lists, group), BF),
            vmem((group, lists), BF),
            vmem((lists, 2 * hid), F32),
            vmem((lists, hid), F32),
            vmem((lists, 2 * hid), BF),
            vmem((lists, hid), BF),
            vmem((nc, cycle - 1, 2, cap, cw), BF),
            vmem((nc, cycle, 2, cap, cw), BF),
            vmem((cycle, 2, 8, cap), F32),
            vmem((cycle - 1, 8, cap), F32),
            vmem((nc, 2, own, cw), F32),
            vmem((nc, 2, own, cw), BF),
            vmem((nc, 2, own, cw), BF),
            vmem((nc, 2, own, cw), BF),
            vmem((nc, cw, 2 * hid), BF),
            vmem((nc, hid, cw), BF),
            dma((2, nc)), dma((2,)), dma((nc,)), dma,
            dma((2, nc)), dma((2, nc)), dma, dma,
            dma((2, nc)), dma((2, nc)), dma((2,)), dma((2,)),
            dma((2, nc)), dma((2, nc)), dma((cycle, 2)), dma((cycle, 2)),
            dma((nc,)), dma((nc,)),
            dma((2, nc)), dma((2, nc)), dma((nc,)),
        ],
        compiler_params=pltpu.CompilerParams(
            collective_id=0, has_side_effects=True, vmem_limit_bytes=60 * 1024 * 1024
        ),
        name="routed_experts",
    )(tokens, cotangent, padded, slot_rows, w_gate, w_up, w_down)
    mixed, in_grad, gates, d_gate, d_up, d_down = outs
    return mixed, in_grad, gates[:, :cycle], d_gate, d_up, d_down


def solution(mesh):
    in_specs = (
        P(("blk", "dp"), None),
        P(("blk", "dp"), None),
        P(("blk", "dp"), None),
        P("blk", None),
        P("blk", None, "dp"),
        P("blk", None, "dp"),
        P("blk", "dp", None),
    )
    out_specs = (
        P(("blk", "dp"), None),
        P(("blk", "dp"), None),
        P(("blk", "dp"), None),
        P("blk", None, "dp"),
        P("blk", None, "dp"),
        P("blk", "dp", None),
    )
    return jax.shard_map(
        on_device, mesh=mesh, in_specs=in_specs, out_specs=out_specs, check_vma=False
    )
```

```python
import jax
import jax.numpy as jnp
from jax import lax
from jax.experimental import pallas as pl
from jax.experimental.pallas import tpu as pltpu
from jax.sharding import PartitionSpec as P

BF = jnp.bfloat16
F32 = jnp.float32
MESH = pl.DeviceIdType.MESH
CHUNKS = 8
AHEAD = 8
LAG = 2
PARTS = 2


def dot(a, b, ca=1, cb=0):
    return lax.dot_general(a, b, (((ca,), (cb,)), ((), ())), preferred_element_type=F32)


def kernel(
    blocks, tok, cot, gate, slots, w_g, w_u, w_d,
    o_mix, o_in, o_gate, o_dg, o_du, o_dd,
    X, E, S, G, EG, GS, WGU, WD, PICK, PUT, PRE, BACK, PGU, HW, R, RR, GG, GGS, OWN, YS, YR, OUT, DGU, DD,
    ld_x, ld_w, ld_d, ld_g, yf_s, yf_r, yg_s, yg_r, xf_s, xf_r, xg_s, xg_r, xr_s, xr_r, gg_s, gg_r, yr_s, yr_r,
    st_o, st_w, st_d,
):
    nc, _, _, cw = X.shape
    own, cap = tok.shape[0], slots.shape[1]
    hid = WD.shape[1]
    b, h = lax.axis_index("blk"), lax.axis_index("dp")
    peer = (b, 1 - h)
    x8 = lax.rem(b, 8)

    def down(s):
        return lax.rem(b + blocks - s, blocks)

    def up(s):
        return lax.rem(b + s, blocks)

    def relayed(c):
        return lax.rem(lax.div(c, 2), 2)

    def down_route(s, c):
        cross = 1 - lax.div(x8 + 8 - s, 8)
        relay = cross * (relayed(c))
        return (down(s + relay * (8 - s)), lax.rem(h + cross * lax.rem(c + s, 2), 2)), s + 2 * relay

    def up_route(s, c):
        cross = lax.div(x8 + s, 8)
        relay = cross * (lax.div(c, nc // 2))
        return (up(s + relay * (8 - s)), lax.rem(h + cross * lax.rem(c + s, 2), 2)), s + 2 * relay

    def cols(c):
        return pl.ds(pl.multiple_of(c * cw, cw), cw)

    def load_x(k, c):
        return pltpu.make_async_copy((tok, cot)[k].at[:, cols(c)], X.at[c, k, pl.ds(0, own)], ld_x.at[k, c])

    def send_y(k, c):
        return pltpu.make_async_remote_copy(
            (tok, cot)[k].at[:, cols(c)], X.at[c, k, pl.ds(own, own)], yf_s.at[k, c], yf_r.at[k, c],
            device_id=peer, device_id_type=MESH)

    def send_x(s, c):
        device, slot = down_route(s, c)
        return pltpu.make_async_remote_copy(
            S.at[c, s - 1], E.at[c, slot], xf_s.at[s - 1, c], xf_r.at[slot - 1, c],
            device_id=device, device_id_type=MESH)

    def take_x(slot, c):
        return pltpu.make_async_remote_copy(
            S.at[c, 0], E.at[c, slot], xf_s.at[0, c], xf_r.at[slot - 1, c], device_id=peer, device_id_type=MESH)

    def relay_x(s, c):
        return pltpu.make_async_remote_copy(
            E.at[c, s + 2], E.at[c, s], xf_s.at[s + 1, c], xf_r.at[s - 1, c],
            device_id=(lax.rem(b + 8 - s, blocks), h), device_id_type=MESH)

    def send_back(s, c):
        device, slot = up_route(s, c)
        return pltpu.make_async_remote_copy(
            R.at[c, s - 1], RR.at[c, slot], xr_s.at[s - 1, c], xr_r.at[slot - 1, c],
            device_id=device, device_id_type=MESH)

    def take_back(slot, c):
        return pltpu.make_async_remote_copy(
            R.at[c, 0], RR.at[c, slot], xr_s.at[0, c], xr_r.at[slot - 1, c], device_id=peer, device_id_type=MESH)

    def relay_back(s, c):
        return pltpu.make_async_remote_copy(
            RR.at[c, s + 2], RR.at[c, s], xr_s.at[s + 1, c], xr_r.at[s - 1, c],
            device_id=(lax.rem(b + blocks - 8 + s, blocks), h), device_id_type=MESH)

    def relays_x(c, act):
        for s in (2, 1):

            @pl.when((1 - lax.div(x8 + 8 - s, 8)) * (relayed(c)) == 1)
            def _():
                act(s, c)

    def relays_back(c, act):
        for s in (2, 1):

            @pl.when(lax.div(x8 + s, 8) * (lax.div(c, nc // 2)) == 1)
            def _():
                act(s, c)

    def pass_x(s, c):
        take_x(s + 2, c).wait_recv()
        relay_x(s, c).start()

    def pass_back(s, c):
        take_back(s + 2, c).wait_recv()
        relay_back(s, c).start()

    def send_sum(c):
        return pltpu.make_async_remote_copy(
            YS.at[c], YR.at[c], yr_s.at[c], yr_r.at[c], device_id=peer, device_id_type=MESH)

    def send_gate():
        return pltpu.make_async_remote_copy(
            gate, G.at[1], yg_s, yg_r, device_id=peer, device_id_type=MESH)

    def send_list_gate(s):
        return pltpu.make_async_remote_copy(
            GS.at[s - 1], EG.at[s], xg_s.at[s - 1], xg_r.at[s - 1],
            device_id=(down(s), h), device_id_type=MESH)

    def send_gate_grad(s, rel):
        source = GG.at[0, 0] if s == 0 else GGS.at[s - 1]
        target = (up(s), h if rel == 0 else 1 - h)
        return pltpu.make_async_remote_copy(
            source, GG.at[s, rel], gg_s.at[s, rel], gg_r.at[s, rel], device_id=target, device_id_type=MESH)

    routes = [(0, 1), (1, 0), (1, 1), (2, 0), (2, 1)]

    bar = pltpu.get_barrier_semaphore()
    near = [peer] + [(f(s), d) for f in (down, up) for s in (1, 2, 8) for d in (h, 1 - h)]
    for device in near:
        pl.semaphore_signal(bar, inc=1, device_id=device, device_id_type=MESH)
    load_gate = pltpu.make_async_copy(gate, G.at[0], ld_g)
    load_gate.start()

    def begin(c, _):
        load_x(0, c).start()
        load_x(1, c).start()
        return 0

    lax.fori_loop(0, nc, begin, 0)
    pl.semaphore_wait(bar, len(near))
    send_gate().start()

    def cross(c, _):
        send_y(0, c).start()
        send_y(1, c).start()
        return 0

    lax.fori_loop(0, 2, cross, 0)
    load_wg = pltpu.make_async_copy(w_g.at[0], WGU.at[:, pl.ds(0, hid)], ld_w.at[0])
    load_wu = pltpu.make_async_copy(w_u.at[0], WGU.at[:, pl.ds(hid, hid)], ld_w.at[1])
    load_wg.start()
    load_wu.start()

    def load_wd(c):
        return pltpu.make_async_copy(w_d.at[0, :, cols(c)], WD.at[c], ld_d.at[c])

    def begin_d(c, _):
        load_wd(c).start()
        return 0

    lax.fori_loop(0, nc, begin_d, 0)

    for s in range(3):
        row = slots[s : s + 1, :]
        at = lax.broadcasted_iota(jnp.int32, (own, cap), 0)
        mine = jnp.where(row == at + h * own, 1.0, 0.0).astype(F32)
        other = jnp.where(row == at + (1 - h) * own, 1.0, 0.0).astype(F32)
        PUT[0:own, s * cap : (s + 1) * cap] = mine.astype(BF)
        PUT[own : 2 * own, s * cap : (s + 1) * cap] = other.astype(BF)
        both = jnp.concatenate([mine, other], axis=0)
        PICK[s * cap : (s + 1) * cap, :] = both.T.astype(BF)
    PRE[...] = jnp.zeros_like(PRE)
    BACK[...] = jnp.zeros_like(BACK)

    load_gate.wait()
    send_gate().wait_recv()
    for s in (2, 1, 0):
        span = slice(s * cap, (s + 1) * cap)
        row = dot(G[0], PUT[0:own, span]) + dot(G[1], PUT[own : 2 * own, span])
        picked = jnp.broadcast_to(row[s : s + 1, :], (cap, cap)).T.astype(BF)
        if s:
            GS[s - 1] = picked
            send_list_gate(s).start()
        else:
            EG[0] = picked
    load_wg.wait()
    load_wu.wait()

    def project(c):
        take_x(1, c).wait_recv()
        take_x(2, c).wait_recv()
        load_wd(c).wait()
        x = E[c, 0:3, 0].reshape(3 * cap, cw)
        dy = E[c, 0:3, 1].reshape(3 * cap, cw)
        PRE[...] += dot(x, WGU[pl.ds(pl.multiple_of(c * cw, cw), cw), :])
        BACK[...] += dot(dy, WD[c], 1, 1)

    def forward(c, _):
        for k in range(2):
            load_x(k, c).wait()
            send_y(k, c).wait_recv()
        for k in range(2):
            rows = dot(PICK[...], X[c, k]).astype(BF)
            E[c, 0, k] = rows[0:cap]
            S[c, 0, k] = rows[cap : 2 * cap]
            S[c, 1, k] = rows[2 * cap : 3 * cap]
        send_x(2, c).start()
        send_x(1, c).start()

        @pl.when(c < nc - 2)
        def _():
            cross(c + 2, 0)

        @pl.when(c > 0)
        def _():
            relays_x(c - 1, pass_x)

        @pl.when(c > 1)
        def _():
            project(c - 2)

        return 0

    lax.fori_loop(0, nc, forward, 0)
    relays_x(nc - 1, pass_x)
    project(nc - 2)
    project(nc - 1)
    send_list_gate(1).wait_recv()
    send_list_gate(2).wait_recv()

    for s in range(3):
        rows = slice(s * cap, (s + 1) * cap)
        gate_col = EG[s].astype(F32)[:, s : s + 1]
        pre_gate = PRE[rows, 0:hid]
        pre_up = PRE[rows, hid : 2 * hid]
        back = BACK[rows, :]
        sig = jax.nn.sigmoid(pre_gate)
        active = pre_gate * sig
        hidden = active * pre_up
        part = jnp.sum(hidden * back, axis=1, keepdims=True)
        part = jnp.broadcast_to(part, (cap, cap)).T[0:8, :]
        if s == 0:
            GG[0, 0] = part
        else:
            GGS[s - 1] = part
        grad = back * gate_col
        HW[rows, :] = (hidden * gate_col).astype(BF)
        PGU[rows, 0:hid] = (grad * pre_up * sig * (1.0 + pre_gate * (1.0 - sig))).astype(BF)
        PGU[rows, hid : 2 * hid] = (grad * active).astype(BF)

    def results(c, _):
        weighted = dot(HW[...], WD[c]).astype(BF)
        in_grad = dot(PGU[...], WGU[pl.ds(pl.multiple_of(c * cw, cw), cw), :], 1, 1).astype(BF)
        for k, value in enumerate((weighted, in_grad)):
            RR[c, 0, k] = value[0:cap]
            R[c, 0, k] = value[cap : 2 * cap]
            R[c, 1, k] = value[2 * cap : 3 * cap]
        send_back(2, c).start()
        send_back(1, c).start()
        return 0

    lax.fori_loop(0, AHEAD, results, 0)
    for s, rel in routes:
        send_gate_grad(s, rel).start()

    def store_w(k, c):
        target = (o_dg, o_du)[k].at[0, pl.ds(pl.multiple_of(c * cw, cw), cw), :]
        return pltpu.make_async_copy(DGU.at[c, :, pl.ds(k * hid, hid)], target, st_w.at[k, c])

    def store_d(c):
        return pltpu.make_async_copy(DD.at[c], o_dd.at[0, :, cols(c)], st_d.at[c])

    def weight_grads(c):
        x = E[c, 0:3, 0].reshape(3 * cap, cw)
        dy = E[c, 0:3, 1].reshape(3 * cap, cw)
        DGU[c] = dot(x, PGU[...], 0, 0).astype(BF)
        DD[c] = dot(HW[...], dy, 0, 0).astype(BF)
        store_w(0, c).start()
        store_w(1, c).start()
        store_d(c).start()

    def store_out(k, c):
        return pltpu.make_async_copy(OUT.at[c, k], (o_mix, o_in)[k].at[:, cols(c)], st_o.at[k, c])

    def finish(c):
        send_sum(c).wait_recv()
        for k in range(2):
            OUT[c, k] = (OWN[c, k] + YR[c, k].astype(F32)).astype(BF)
            store_out(k, c).start()

    def collect(c, _):
        @pl.when(c < nc - AHEAD)
        def _():
            results(c + AHEAD, 0)

        relays_back(c, pass_back)
        take_back(1, c).wait_recv()
        take_back(2, c).wait_recv()
        for k in range(2):
            rows = RR[c, 0:3, k].reshape(3 * cap, cw)
            total = dot(PUT[...], rows)
            YS[c, k] = total[own : 2 * own].astype(BF)
            OWN[c, k] = total[0:own]
        send_sum(c).start()

        weight_grads(c)

        @pl.when(c >= LAG)
        def _():
            finish(c - LAG)

        return 0

    lax.fori_loop(0, nc, collect, 0)

    for s, rel in routes:
        send_gate_grad(s, rel).wait_recv()
    lane = lax.broadcasted_iota(jnp.int32, (own, cap), 1)
    grads = jnp.zeros((own, cap), F32)
    for s in range(3):
        row = GG[s, 0][0:1, :] + GG[s, 1][0:1, :]
        named = PUT[0:own, s * cap : (s + 1) * cap].astype(F32)
        column = jnp.sum(jnp.where(named > 0.5, jnp.broadcast_to(row, (own, cap)), 0.0), axis=1, keepdims=True)
        grads = jnp.where(lane == s, column, grads)
    o_gate[...] = grads.T[0:3, :]

    def finish_last(c, _):
        finish(c)
        return 0

    lax.fori_loop(nc - LAG, nc, finish_last, 0)

    send_gate().wait_send()
    for s in (1, 2):
        send_list_gate(s).wait_send()
    for s, rel in routes:
        send_gate_grad(s, rel).wait_send()

    def drain(c, _):
        for k in range(2):
            send_y(k, c).wait_send()
            store_w(k, c).wait()
            store_out(k, c).wait()
        for s in (1, 2):
            send_x(s, c).wait_send()
            send_back(s, c).wait_send()
        send_sum(c).wait_send()
        store_d(c).wait()
        relays_x(c, lambda s, c: relay_x(s, c).wait_send())
        relays_back(c, lambda s, c: relay_back(s, c).wait_send())
        return 0

    lax.fori_loop(0, nc, drain, 0)


def hand_out(arrays):
    big = [i for i, a in enumerate(arrays) if a.size > 4096]

    def body(*refs):
        n = len(arrays)
        src, dst, hold = refs[:n], refs[n : 2 * n], refs[2 * n : 2 * n + len(big)]
        rd, wr = refs[-2], refs[-1]
        pieces = []
        for j, i in enumerate(big):
            ref = (src[i], dst[i], hold[j])
            if len(ref[0].shape) == 3:
                ref = (ref[0].at[0], ref[1].at[0], ref[2].at[0])
            rows = ref[0].shape[0] // PARTS
            for p in range(PARTS):
                at = pl.ds(p * rows, rows)
                read = pltpu.make_async_copy(ref[0].at[at], ref[2].at[at], rd.at[j, p])
                write = pltpu.make_async_copy(ref[2].at[at], ref[1].at[at], wr.at[j, p])
                pieces.append((read, write))
        for read, _ in pieces:
            read.start()
        for i in range(n):
            if i not in big:
                dst[i][...] = src[i][...]
        for read, write in pieces:
            read.wait()
            write.start()
        for _, write in pieces:
            write.wait()

    specs = [pl.BlockSpec(memory_space=pl.ANY if i in big else pltpu.VMEM) for i in range(len(arrays))]
    return pl.pallas_call(
        body,
        out_shape=tuple(jax.ShapeDtypeStruct(a.shape, a.dtype) for a in arrays),
        in_specs=specs,
        out_specs=tuple(specs),
        scratch_shapes=[pltpu.VMEM(arrays[i].shape, arrays[i].dtype) for i in big]
        + [pltpu.SemaphoreType.DMA((len(big), PARTS))] * 2,
        compiler_params=pltpu.CompilerParams(vmem_limit_bytes=60 * 1024 * 1024),
        name="hand_out",
    )(*arrays)


def on_device(tokens, cotangent, gate_probs, slot_rows, w_gate, w_up, w_down):
    own, width = tokens.shape
    cycle, cap = slot_rows.shape
    hid = w_gate.shape[2]
    nc, cw = CHUNKS, width // CHUNKS
    group, lists = 2 * own, cycle * cap
    blocks = lax.axis_size("blk")
    hops = 2 * (cycle - 1)
    dma = pltpu.SemaphoreType.DMA
    vmem = pltpu.VMEM
    any_space = pl.BlockSpec(memory_space=pl.ANY)
    in_vmem = pl.BlockSpec(memory_space=pltpu.VMEM)

    def body(*refs):
        kernel(blocks, *refs)

    outs = pl.pallas_call(
        body,
        out_shape=(
            jax.ShapeDtypeStruct((own, width), BF),
            jax.ShapeDtypeStruct((own, width), BF),
            jax.ShapeDtypeStruct((cycle, own), F32),
            jax.ShapeDtypeStruct(w_gate.shape, BF),
            jax.ShapeDtypeStruct(w_up.shape, BF),
            jax.ShapeDtypeStruct(w_down.shape, BF),
        ),
        in_specs=[any_space, any_space, any_space, in_vmem, any_space, any_space, any_space],
        out_specs=(any_space, any_space, in_vmem, any_space, any_space, any_space),
        scratch_shapes=[
            vmem((nc, 2, group, cw), BF),
            vmem((nc, 1 + hops, 2, cap, cw), BF),
            vmem((nc, cycle - 1, 2, cap, cw), BF),
            vmem((2, cycle, own), BF),
            vmem((cycle, cap, cap), BF),
            vmem((cycle - 1, cap, cap), BF),
            vmem((width, 2 * hid), BF),
            vmem((nc, hid, cw), BF),
            vmem((lists, group), BF),
            vmem((group, lists), BF),
            vmem((lists, 2 * hid), F32),
            vmem((lists, hid), F32),
            vmem((lists, 2 * hid), BF),
            vmem((lists, hid), BF),
            vmem((nc, cycle - 1, 2, cap, cw), BF),
            vmem((nc, 1 + hops, 2, cap, cw), BF),
            vmem((cycle, 2, 8, cap), F32),
            vmem((cycle - 1, 8, cap), F32),
            vmem((nc, 2, own, cw), F32),
            vmem((nc, 2, own, cw), BF),
            vmem((nc, 2, own, cw), BF),
            vmem((nc, 2, own, cw), BF),
            vmem((nc, cw, 2 * hid), BF),
            vmem((nc, hid, cw), BF),
            dma((2, nc)), dma((2,)), dma((nc,)), dma,
            dma((2, nc)), dma((2, nc)), dma, dma,
            dma((hops, nc)), dma((hops, nc)), dma((2,)), dma((2,)),
            dma((hops, nc)), dma((hops, nc)), dma((cycle, 2)), dma((cycle, 2)),
            dma((nc,)), dma((nc,)),
            dma((2, nc)), dma((2, nc)), dma((nc,)),
        ],
        compiler_params=pltpu.CompilerParams(
            collective_id=0, has_side_effects=True, vmem_limit_bytes=60 * 1024 * 1024
        ),
        name="routed_experts",
    )(tokens, cotangent, gate_probs.T, slot_rows, w_gate, w_up, w_down)
    mixed, in_grad, gates, d_gate, d_up, d_down = hand_out(outs)
    return mixed, in_grad, gates.T, d_gate, d_up, d_down


def solution(mesh):
    in_specs = (
        P(("blk", "dp"), None),
        P(("blk", "dp"), None),
        P(("blk", "dp"), None),
        P("blk", None),
        P("blk", None, "dp"),
        P("blk", None, "dp"),
        P("blk", "dp", None),
    )
    out_specs = (
        P(("blk", "dp"), None),
        P(("blk", "dp"), None),
        P(("blk", "dp"), None),
        P("blk", None, "dp"),
        P("blk", None, "dp"),
        P("blk", "dp", None),
    )
    return jax.shard_map(
        on_device, mesh=mesh, in_specs=in_specs, out_specs=out_specs, check_vma=False
    )
```

```python
import jax
import jax.numpy as jnp
from jax import lax
from jax.experimental import pallas as pl
from jax.experimental.pallas import tpu as pltpu
from jax.sharding import PartitionSpec as P

BF = jnp.bfloat16
F32 = jnp.float32
MESH = pl.DeviceIdType.MESH
CHUNKS = 8
AHEAD = 8
LAG = 2
RELAY_LAG = 2
PROJECT_LAG = 4


def dot(a, b, ca=1, cb=0):
    return lax.dot_general(a, b, (((ca,), (cb,)), ((), ())), preferred_element_type=F32)


def kernel(
    blocks, tok, cot, gate, slots, w_g, w_u, w_d,
    o_mix, o_in, o_gate, o_dg, o_du, o_dd,
    X, E, S, G, EG, GS, WGU, WD, PICK, PUT, PRE, BACK, PGU, HW, R, RR, GG, GGS, OWN, YS, YR, OUT, DGU, DD,
    ld_x, ld_w, ld_d, ld_g, yf_s, yf_r, yg_s, yg_r, xf_s, xf_r, xg_s, xg_r, xr_s, xr_r, gg_s, gg_r, yr_s, yr_r,
    st_o, st_w, st_d,
):
    nc, _, _, cw = X.shape
    own, cap = tok.shape[0], slots.shape[1]
    hid = WD.shape[1]
    b, h = lax.axis_index("blk"), lax.axis_index("dp")
    peer = (b, 1 - h)
    x8 = lax.rem(b, 8)

    def down(s):
        return lax.rem(b + blocks - s, blocks)

    def up(s):
        return lax.rem(b + s, blocks)

    def turn_x(c):
        return lax.rem(c, 4)

    def turn_back(c):
        return lax.div(c, nc // 4) + lax.div(c, nc // 2) - 2 * lax.div(c, 3 * (nc // 4))

    def down_route(s, c):
        cross = 1 - lax.div(x8 + 8 - s, 8)
        turn = turn_x(c)
        relay = cross * lax.div(turn + 3, 4)
        plane = lax.rem(h + cross * lax.rem(lax.div(c, 4) + s, 2), 2)
        return (down(s + relay * (10 - 2 * turn - s)), plane), s + 2 * relay

    def up_route(s, c):
        cross = lax.div(x8 + s, 8)
        turn = turn_back(c)
        relay = cross * lax.div(turn + 3, 4)
        plane = lax.rem(h + cross * lax.rem(c + s, 2), 2)
        return (up(s + relay * (10 - 2 * turn - s)), plane), s + 2 * relay

    def cols(c):
        return pl.ds(pl.multiple_of(c * cw, cw), cw)

    def load_x(k, c):
        return pltpu.make_async_copy((tok, cot)[k].at[:, cols(c)], X.at[c, k, pl.ds(0, own)], ld_x.at[k, c])

    def send_y(k, c):
        return pltpu.make_async_remote_copy(
            (tok, cot)[k].at[:, cols(c)], X.at[c, k, pl.ds(own, own)], yf_s.at[k, c], yf_r.at[k, c],
            device_id=peer, device_id_type=MESH)

    def send_x(s, c):
        device, slot = down_route(s, c)
        return pltpu.make_async_remote_copy(
            S.at[c, s - 1], E.at[c, slot], xf_s.at[s - 1, c], xf_r.at[slot - 1, c],
            device_id=device, device_id_type=MESH)

    def take_x(slot, c):
        return pltpu.make_async_remote_copy(
            S.at[c, 0], E.at[c, slot], xf_s.at[0, c], xf_r.at[slot - 1, c], device_id=peer, device_id_type=MESH)

    def relay_x(s, c):
        return pltpu.make_async_remote_copy(
            E.at[c, s + 2], E.at[c, s], xf_s.at[s + 1, c], xf_r.at[s - 1, c],
            device_id=(lax.rem(b + blocks + 10 - 2 * turn_x(c) - s, blocks), h), device_id_type=MESH)

    def send_back(s, c):
        device, slot = up_route(s, c)
        return pltpu.make_async_remote_copy(
            R.at[c, s - 1], RR.at[c, slot], xr_s.at[s - 1, c], xr_r.at[slot - 1, c],
            device_id=device, device_id_type=MESH)

    def take_back(slot, c):
        return pltpu.make_async_remote_copy(
            R.at[c, 0], RR.at[c, slot], xr_s.at[0, c], xr_r.at[slot - 1, c], device_id=peer, device_id_type=MESH)

    def relay_back(s, c):
        return pltpu.make_async_remote_copy(
            RR.at[c, s + 2], RR.at[c, s], xr_s.at[s + 1, c], xr_r.at[s - 1, c],
            device_id=(lax.rem(b + blocks - 10 + 2 * turn_back(c) + s, blocks), h), device_id_type=MESH)

    def relays_x(c, act):
        for s in (2, 1):

            core = x8 - 2 * (turn_x(c) - 1)

            @pl.when((turn_x(c) > 0) & (core >= 0) & (core < s))
            def _():
                act(s, c)

    def relays_back(c, act):
        for s in (2, 1):

            core = x8 - 8 + 2 * turn_back(c)

            @pl.when((turn_back(c) > 0) & (core <= 1) & (core >= 2 - s))
            def _():
                act(s, c)

    def pass_x(s, c):
        take_x(s + 2, c).wait_recv()
        relay_x(s, c).start()

    def pass_back(s, c):
        take_back(s + 2, c).wait_recv()
        relay_back(s, c).start()

    def send_sum(c):
        return pltpu.make_async_remote_copy(
            YS.at[c], YR.at[c], yr_s.at[c], yr_r.at[c], device_id=peer, device_id_type=MESH)

    def send_gate():
        return pltpu.make_async_remote_copy(
            gate, G.at[1], yg_s, yg_r, device_id=peer, device_id_type=MESH)

    def send_list_gate(s):
        return pltpu.make_async_remote_copy(
            GS.at[s - 1], EG.at[s], xg_s.at[s - 1], xg_r.at[s - 1],
            device_id=(down(s), h), device_id_type=MESH)

    def send_gate_grad(s, rel):
        source = GG.at[0, 0] if s == 0 else GGS.at[s - 1]
        target = (up(s), h if rel == 0 else 1 - h)
        return pltpu.make_async_remote_copy(
            source, GG.at[s, rel], gg_s.at[s, rel], gg_r.at[s, rel], device_id=target, device_id_type=MESH)

    routes = [(0, 1), (1, 0), (1, 1), (2, 0), (2, 1)]

    bar = pltpu.get_barrier_semaphore()
    near = [peer] + [(f(s), d) for f in (down, up) for s in (1, 2, 4, 6, 8) for d in (h, 1 - h)]
    for device in near:
        pl.semaphore_signal(bar, inc=1, device_id=device, device_id_type=MESH)
    load_gate = pltpu.make_async_copy(gate, G.at[0], ld_g)
    load_gate.start()

    def begin(c, _):
        load_x(0, c).start()
        load_x(1, c).start()
        return 0

    lax.fori_loop(0, nc, begin, 0)
    pl.semaphore_wait(bar, len(near))
    send_gate().start()

    def cross(c, _):
        send_y(0, c).start()
        send_y(1, c).start()
        return 0

    lax.fori_loop(0, 2, cross, 0)
    load_wg = pltpu.make_async_copy(w_g.at[0], WGU.at[:, pl.ds(0, hid)], ld_w.at[0])
    load_wu = pltpu.make_async_copy(w_u.at[0], WGU.at[:, pl.ds(hid, hid)], ld_w.at[1])
    load_wg.start()
    load_wu.start()

    def load_wd(c):
        return pltpu.make_async_copy(w_d.at[0, :, cols(c)], WD.at[c], ld_d.at[c])

    def begin_d(c, _):
        load_wd(c).start()
        return 0

    lax.fori_loop(0, nc, begin_d, 0)

    for s in range(3):
        row = slots[s : s + 1, :]
        at = lax.broadcasted_iota(jnp.int32, (own, cap), 0)
        mine = jnp.where(row == at + h * own, 1.0, 0.0).astype(F32)
        other = jnp.where(row == at + (1 - h) * own, 1.0, 0.0).astype(F32)
        PUT[0:own, s * cap : (s + 1) * cap] = mine.astype(BF)
        PUT[own : 2 * own, s * cap : (s + 1) * cap] = other.astype(BF)
        both = jnp.concatenate([mine, other], axis=0)
        PICK[s * cap : (s + 1) * cap, :] = both.T.astype(BF)
    PRE[...] = jnp.zeros_like(PRE)
    BACK[...] = jnp.zeros_like(BACK)

    load_gate.wait()
    send_gate().wait_recv()
    for s in (2, 1, 0):
        span = slice(s * cap, (s + 1) * cap)
        row = dot(G[0], PUT[0:own, span]) + dot(G[1], PUT[own : 2 * own, span])
        picked = jnp.broadcast_to(row[s : s + 1, :], (cap, cap)).T.astype(BF)
        if s:
            GS[s - 1] = picked
            send_list_gate(s).start()
        else:
            EG[0] = picked
    load_wg.wait()
    load_wu.wait()

    def project(c):
        take_x(1, c).wait_recv()
        take_x(2, c).wait_recv()
        load_wd(c).wait()
        x = E[c, 0:3, 0].reshape(3 * cap, cw)
        dy = E[c, 0:3, 1].reshape(3 * cap, cw)
        PRE[...] += dot(x, WGU[pl.ds(pl.multiple_of(c * cw, cw), cw), :])
        BACK[...] += dot(dy, WD[c], 1, 1)

    def forward(c, _):
        for k in range(2):
            load_x(k, c).wait()
            send_y(k, c).wait_recv()
        for k in range(2):
            rows = dot(PICK[...], X[c, k]).astype(BF)
            E[c, 0, k] = rows[0:cap]
            S[c, 0, k] = rows[cap : 2 * cap]
            S[c, 1, k] = rows[2 * cap : 3 * cap]
        send_x(2, c).start()
        send_x(1, c).start()

        @pl.when(c < nc - 2)
        def _():
            cross(c + 2, 0)

        @pl.when(c >= RELAY_LAG)
        def _():
            relays_x(c - RELAY_LAG, pass_x)

        @pl.when(c >= PROJECT_LAG)
        def _():
            project(c - PROJECT_LAG)

        return 0

    lax.fori_loop(0, nc, forward, 0)
    for c in range(nc - RELAY_LAG, nc):
        relays_x(c, pass_x)

    def project_last(c, _):
        project(c)
        return 0

    lax.fori_loop(nc - PROJECT_LAG, nc, project_last, 0)
    send_list_gate(1).wait_recv()
    send_list_gate(2).wait_recv()

    for s in range(3):
        rows = slice(s * cap, (s + 1) * cap)
        gate_col = EG[s].astype(F32)[:, s : s + 1]
        pre_gate = PRE[rows, 0:hid]
        pre_up = PRE[rows, hid : 2 * hid]
        back = BACK[rows, :]
        sig = jax.nn.sigmoid(pre_gate)
        active = pre_gate * sig
        hidden = active * pre_up
        part = jnp.sum(hidden * back, axis=1, keepdims=True)
        part = jnp.broadcast_to(part, (cap, cap)).T[0:8, :]
        if s == 0:
            GG[0, 0] = part
        else:
            GGS[s - 1] = part
        grad = back * gate_col
        HW[rows, :] = (hidden * gate_col).astype(BF)
        PGU[rows, 0:hid] = (grad * pre_up * sig * (1.0 + pre_gate * (1.0 - sig))).astype(BF)
        PGU[rows, hid : 2 * hid] = (grad * active).astype(BF)

    def results(c, _):
        weighted = dot(HW[...], WD[c]).astype(BF)
        in_grad = dot(PGU[...], WGU[pl.ds(pl.multiple_of(c * cw, cw), cw), :], 1, 1).astype(BF)
        for k, value in enumerate((weighted, in_grad)):
            RR[c, 0, k] = value[0:cap]
            R[c, 0, k] = value[cap : 2 * cap]
            R[c, 1, k] = value[2 * cap : 3 * cap]
        send_back(2, c).start()
        send_back(1, c).start()
        return 0

    lax.fori_loop(0, AHEAD, results, 0)
    for s, rel in routes:
        send_gate_grad(s, rel).start()

    def store_w(k, c):
        target = (o_dg, o_du)[k].at[0, pl.ds(pl.multiple_of(c * cw, cw), cw), :]
        return pltpu.make_async_copy(DGU.at[c, :, pl.ds(k * hid, hid)], target, st_w.at[k, c])

    def store_d(c):
        return pltpu.make_async_copy(DD.at[c], o_dd.at[0, :, cols(c)], st_d.at[c])

    def weight_grads(c):
        x = E[c, 0:3, 0].reshape(3 * cap, cw)
        dy = E[c, 0:3, 1].reshape(3 * cap, cw)
        DGU[c] = dot(x, PGU[...], 0, 0).astype(BF)
        DD[c] = dot(HW[...], dy, 0, 0).astype(BF)
        store_w(0, c).start()
        store_w(1, c).start()
        store_d(c).start()

    def store_out(k, c):
        return pltpu.make_async_copy(OUT.at[c, k], (o_mix, o_in)[k].at[:, cols(c)], st_o.at[k, c])

    def finish(c):
        send_sum(c).wait_recv()
        for k in range(2):
            OUT[c, k] = (OWN[c, k] + YR[c, k].astype(F32)).astype(BF)
            store_out(k, c).start()

    def collect(c, _):
        @pl.when(c < nc - AHEAD)
        def _():
            results(c + AHEAD, 0)

        relays_back(c, pass_back)
        take_back(1, c).wait_recv()
        take_back(2, c).wait_recv()
        for k in range(2):
            rows = RR[c, 0:3, k].reshape(3 * cap, cw)
            total = dot(PUT[...], rows)
            YS[c, k] = total[own : 2 * own].astype(BF)
            OWN[c, k] = total[0:own]
        send_sum(c).start()

        weight_grads(c)

        @pl.when(c >= LAG)
        def _():
            finish(c - LAG)

        return 0

    lax.fori_loop(0, nc, collect, 0)

    for s, rel in routes:
        send_gate_grad(s, rel).wait_recv()
    lane = lax.broadcasted_iota(jnp.int32, (own, cap), 1)
    grads = jnp.zeros((own, cap), F32)
    for s in range(3):
        row = GG[s, 0][0:1, :] + GG[s, 1][0:1, :]
        named = PUT[0:own, s * cap : (s + 1) * cap].astype(F32)
        column = jnp.sum(jnp.where(named > 0.5, jnp.broadcast_to(row, (own, cap)), 0.0), axis=1, keepdims=True)
        grads = jnp.where(lane == s, column, grads)
    o_gate[...] = grads.T[0:3, :]

    def finish_last(c, _):
        finish(c)
        return 0

    lax.fori_loop(nc - LAG, nc, finish_last, 0)

    send_gate().wait_send()
    for s in (1, 2):
        send_list_gate(s).wait_send()
    for s, rel in routes:
        send_gate_grad(s, rel).wait_send()

    def drain(c, _):
        for k in range(2):
            send_y(k, c).wait_send()
            store_w(k, c).wait()
            store_out(k, c).wait()
        for s in (1, 2):
            send_x(s, c).wait_send()
            send_back(s, c).wait_send()
        send_sum(c).wait_send()
        store_d(c).wait()
        relays_x(c, lambda s, c: relay_x(s, c).wait_send())
        relays_back(c, lambda s, c: relay_back(s, c).wait_send())
        return 0

    lax.fori_loop(0, nc, drain, 0)


def hand_out(arrays):
    big = [i for i, a in enumerate(arrays) if a.size > 4096]

    def body(*refs):
        n = len(arrays)
        src, dst = refs[:n], refs[n : 2 * n]
        wr = refs[-1]
        copies = [pltpu.make_async_copy(src[i], dst[i], wr.at[j]) for j, i in enumerate(big)]
        for copy in copies:
            copy.start()
        for i in range(n):
            if i not in big:
                dst[i][...] = src[i][...]
        for copy in copies:
            copy.wait()

    specs = [pl.BlockSpec(memory_space=pl.ANY if i in big else pltpu.VMEM) for i in range(len(arrays))]
    return pl.pallas_call(
        body,
        out_shape=tuple(jax.ShapeDtypeStruct(a.shape, a.dtype) for a in arrays),
        in_specs=specs,
        out_specs=tuple(specs),
        scratch_shapes=[pltpu.SemaphoreType.DMA((len(big),))],
        compiler_params=pltpu.CompilerParams(vmem_limit_bytes=1024 * 1024),
        name="hand_out",
    )(*arrays)


def on_device(tokens, cotangent, gate_probs, slot_rows, w_gate, w_up, w_down):
    own, width = tokens.shape
    cycle, cap = slot_rows.shape
    hid = w_gate.shape[2]
    nc, cw = CHUNKS, width // CHUNKS
    group, lists = 2 * own, cycle * cap
    blocks = lax.axis_size("blk")
    hops = 2 * (cycle - 1)
    dma = pltpu.SemaphoreType.DMA
    vmem = pltpu.VMEM
    any_space = pl.BlockSpec(memory_space=pl.ANY)
    in_vmem = pl.BlockSpec(memory_space=pltpu.VMEM)

    def body(*refs):
        kernel(blocks, *refs)

    outs = pl.pallas_call(
        body,
        out_shape=(
            jax.ShapeDtypeStruct((own, width), BF),
            jax.ShapeDtypeStruct((own, width), BF),
            jax.ShapeDtypeStruct((cycle, own), F32),
            jax.ShapeDtypeStruct(w_gate.shape, BF),
            jax.ShapeDtypeStruct(w_up.shape, BF),
            jax.ShapeDtypeStruct(w_down.shape, BF),
        ),
        in_specs=[any_space, any_space, any_space, in_vmem, any_space, any_space, any_space],
        out_specs=(any_space, any_space, in_vmem, any_space, any_space, any_space),
        scratch_shapes=[
            vmem((nc, 2, group, cw), BF),
            vmem((nc, 1 + hops, 2, cap, cw), BF),
            vmem((nc, cycle - 1, 2, cap, cw), BF),
            vmem((2, cycle, own), BF),
            vmem((cycle, cap, cap), BF),
            vmem((cycle - 1, cap, cap), BF),
            vmem((width, 2 * hid), BF),
            vmem((nc, hid, cw), BF),
            vmem((lists, group), BF),
            vmem((group, lists), BF),
            vmem((lists, 2 * hid), F32),
            vmem((lists, hid), F32),
            vmem((lists, 2 * hid), BF),
            vmem((lists, hid), BF),
            vmem((nc, cycle - 1, 2, cap, cw), BF),
            vmem((nc, 1 + hops, 2, cap, cw), BF),
            vmem((cycle, 2, 8, cap), F32),
            vmem((cycle - 1, 8, cap), F32),
            vmem((nc, 2, own, cw), F32),
            vmem((nc, 2, own, cw), BF),
            vmem((nc, 2, own, cw), BF),
            vmem((nc, 2, own, cw), BF),
            vmem((nc, cw, 2 * hid), BF),
            vmem((nc, hid, cw), BF),
            dma((2, nc)), dma((2,)), dma((nc,)), dma,
            dma((2, nc)), dma((2, nc)), dma, dma,
            dma((hops, nc)), dma((hops, nc)), dma((2,)), dma((2,)),
            dma((hops, nc)), dma((hops, nc)), dma((cycle, 2)), dma((cycle, 2)),
            dma((nc,)), dma((nc,)),
            dma((2, nc)), dma((2, nc)), dma((nc,)),
        ],
        compiler_params=pltpu.CompilerParams(
            collective_id=0, has_side_effects=True, vmem_limit_bytes=46 * 1024 * 1024
        ),
        name="routed_experts",
    )(tokens, cotangent, gate_probs.T, slot_rows, w_gate, w_up, w_down)
    mixed, in_grad, gates, d_gate, d_up, d_down = hand_out(outs)
    return mixed, in_grad, gates.T, d_gate, d_up, d_down


def solution(mesh):
    in_specs = (
        P(("blk", "dp"), None),
        P(("blk", "dp"), None),
        P(("blk", "dp"), None),
        P("blk", None),
        P("blk", None, "dp"),
        P("blk", None, "dp"),
        P("blk", "dp", None),
    )
    out_specs = (
        P(("blk", "dp"), None),
        P(("blk", "dp"), None),
        P(("blk", "dp"), None),
        P("blk", None, "dp"),
        P("blk", None, "dp"),
        P("blk", "dp", None),
    )
    return jax.shard_map(
        on_device, mesh=mesh, in_specs=in_specs, out_specs=out_specs, check_vma=False
    )
```

```python
import jax
import jax.numpy as jnp
from jax import lax
from jax.experimental import pallas as pl
from jax.experimental.pallas import tpu as pltpu
from jax.sharding import PartitionSpec as P

BF = jnp.bfloat16
F32 = jnp.float32
MESH = pl.DeviceIdType.MESH
CHUNKS = 8
AHEAD = 8
LAG = 2
RELAY_LAG = 2
PROJECT_LAG = 4


def dot(a, b, ca=1, cb=0):
    return lax.dot_general(a, b, (((ca,), (cb,)), ((), ())), preferred_element_type=F32)


def kernel(
    blocks, tok, cot, gate, slots, w_g, w_u, w_d,
    o_mix, o_in, o_gate, o_dg, o_du, o_dd,
    X, E, S, G, EG, GS, WGU, WD, PICK, PUT, PRE, BACK, PGU, HW, R, RR, GG, GGS, OWN, YS, YR, OUT, DGU, DD,
    ld_x, ld_w, ld_d, ld_g, yf_s, yf_r, yg_s, yg_r, xf_s, xf_r, xg_s, xg_r, xr_s, xr_r, gg_s, gg_r, yr_s, yr_r,
    st_o, st_w, st_d,
):
    nc, _, _, cw = X.shape
    own, cap = tok.shape[0], slots.shape[1]
    hid = WD.shape[1]
    b, h = lax.axis_index("blk"), lax.axis_index("dp")
    peer = (b, 1 - h)
    x8 = lax.rem(b, 8)

    def down(s):
        return lax.rem(b + blocks - s, blocks)

    def up(s):
        return lax.rem(b + s, blocks)

    def turn_x(c):
        return lax.rem(c, 4)

    def turn_back(c):
        return lax.div(c, nc // 4) + lax.div(c, nc // 2) - 2 * lax.div(c, 3 * (nc // 4))

    def down_route(s, c):
        cross = 1 - lax.div(x8 + 8 - s, 8)
        turn = turn_x(c)
        relay = cross * lax.div(turn + 3, 4)
        plane = lax.rem(h + cross * lax.rem(lax.div(c, 4) + s, 2), 2)
        return (down(s + relay * (10 - 2 * turn - s)), plane), s + 2 * relay

    def up_route(s, c):
        cross = lax.div(x8 + s, 8)
        turn = turn_back(c)
        relay = cross * lax.div(turn + 3, 4)
        plane = lax.rem(h + cross * lax.rem(c + s, 2), 2)
        return (up(s + relay * (10 - 2 * turn - s)), plane), s + 2 * relay

    def cols(c):
        return pl.ds(pl.multiple_of(c * cw, cw), cw)

    def load_x(k, c):
        return pltpu.make_async_copy((tok, cot)[k].at[:, cols(c)], X.at[c, k, pl.ds(0, own)], ld_x.at[k, c])

    def send_y(k, c):
        return pltpu.make_async_remote_copy(
            (tok, cot)[k].at[:, cols(c)], X.at[c, k, pl.ds(own, own)], yf_s.at[k, c], yf_r.at[k, c],
            device_id=peer, device_id_type=MESH)

    def send_x(s, c):
        device, slot = down_route(s, c)
        return pltpu.make_async_remote_copy(
            S.at[c, s - 1], E.at[c, slot], xf_s.at[s - 1, c], xf_r.at[slot - 1, c],
            device_id=device, device_id_type=MESH)

    def take_x(slot, c):
        return pltpu.make_async_remote_copy(
            S.at[c, 0], E.at[c, slot], xf_s.at[0, c], xf_r.at[slot - 1, c], device_id=peer, device_id_type=MESH)

    def relay_x(s, c):
        return pltpu.make_async_remote_copy(
            E.at[c, s + 2], E.at[c, s], xf_s.at[s + 1, c], xf_r.at[s - 1, c],
            device_id=(lax.rem(b + blocks + 10 - 2 * turn_x(c) - s, blocks), h), device_id_type=MESH)

    def send_back(s, c):
        device, slot = up_route(s, c)
        return pltpu.make_async_remote_copy(
            R.at[c, s - 1], RR.at[c, slot], xr_s.at[s - 1, c], xr_r.at[slot - 1, c],
            device_id=device, device_id_type=MESH)

    def take_back(slot, c):
        return pltpu.make_async_remote_copy(
            R.at[c, 0], RR.at[c, slot], xr_s.at[0, c], xr_r.at[slot - 1, c], device_id=peer, device_id_type=MESH)

    def relay_back(s, c):
        return pltpu.make_async_remote_copy(
            RR.at[c, s + 2], RR.at[c, s], xr_s.at[s + 1, c], xr_r.at[s - 1, c],
            device_id=(lax.rem(b + blocks - 10 + 2 * turn_back(c) + s, blocks), h), device_id_type=MESH)

    def relays_x(c, act):
        for s in (2, 1):

            core = x8 - 2 * (turn_x(c) - 1)

            @pl.when((turn_x(c) > 0) & (core >= 0) & (core < s))
            def _():
                act(s, c)

    def relays_back(c, act):
        for s in (2, 1):

            core = x8 - 8 + 2 * turn_back(c)

            @pl.when((turn_back(c) > 0) & (core <= 1) & (core >= 2 - s))
            def _():
                act(s, c)

    def pass_x(s, c):
        take_x(s + 2, c).wait_recv()
        relay_x(s, c).start()

    def pass_back(s, c):
        take_back(s + 2, c).wait_recv()
        relay_back(s, c).start()

    def send_sum(c):
        return pltpu.make_async_remote_copy(
            YS.at[c], YR.at[c], yr_s.at[c], yr_r.at[c], device_id=peer, device_id_type=MESH)

    def send_gate():
        return pltpu.make_async_remote_copy(
            gate, G.at[1], yg_s, yg_r, device_id=peer, device_id_type=MESH)

    def send_list_gate(s):
        return pltpu.make_async_remote_copy(
            GS.at[s - 1], EG.at[s], xg_s.at[s - 1], xg_r.at[s - 1],
            device_id=(down(s), h), device_id_type=MESH)

    def send_gate_grad(s, rel):
        source = GG.at[0, 0] if s == 0 else GGS.at[s - 1]
        target = (up(s), h if rel == 0 else 1 - h)
        return pltpu.make_async_remote_copy(
            source, GG.at[s, rel], gg_s.at[s, rel], gg_r.at[s, rel], device_id=target, device_id_type=MESH)

    routes = [(0, 1), (1, 0), (1, 1), (2, 0), (2, 1)]

    bar = pltpu.get_barrier_semaphore()
    near = [peer] + [(f(s), d) for f in (down, up) for s in (1, 2, 4, 6, 8) for d in (h, 1 - h)]
    for device in near:
        pl.semaphore_signal(bar, inc=1, device_id=device, device_id_type=MESH)
    load_gate = pltpu.make_async_copy(gate, G.at[0], ld_g)
    load_gate.start()

    def begin(c, _):
        load_x(0, c).start()
        load_x(1, c).start()
        return 0

    lax.fori_loop(0, nc, begin, 0)
    pl.semaphore_wait(bar, len(near))
    send_gate().start()

    def cross(c, _):
        send_y(0, c).start()
        send_y(1, c).start()
        return 0

    lax.fori_loop(0, 2, cross, 0)
    load_wg = pltpu.make_async_copy(w_g.at[0], WGU.at[:, pl.ds(0, hid)], ld_w.at[0])
    load_wu = pltpu.make_async_copy(w_u.at[0], WGU.at[:, pl.ds(hid, hid)], ld_w.at[1])
    load_wg.start()
    load_wu.start()

    def load_wd(c):
        return pltpu.make_async_copy(w_d.at[0, :, cols(c)], WD.at[c], ld_d.at[c])

    def begin_d(c, _):
        load_wd(c).start()
        return 0

    lax.fori_loop(0, nc, begin_d, 0)

    for s in range(3):
        row = slots[s : s + 1, :]
        at = lax.broadcasted_iota(jnp.int32, (own, cap), 0)
        mine = jnp.where(row == at + h * own, 1.0, 0.0).astype(F32)
        other = jnp.where(row == at + (1 - h) * own, 1.0, 0.0).astype(F32)
        PUT[0:own, s * cap : (s + 1) * cap] = mine.astype(BF)
        PUT[own : 2 * own, s * cap : (s + 1) * cap] = other.astype(BF)
        both = jnp.concatenate([mine, other], axis=0)
        PICK[s * cap : (s + 1) * cap, :] = both.T.astype(BF)
    PRE[...] = jnp.zeros_like(PRE)
    BACK[...] = jnp.zeros_like(BACK)

    load_gate.wait()
    send_gate().wait_recv()
    for s in (2, 1, 0):
        span = slice(s * cap, (s + 1) * cap)
        row = dot(G[0], PUT[0:own, span]) + dot(G[1], PUT[own : 2 * own, span])
        picked = jnp.broadcast_to(row[s : s + 1, :], (cap, cap)).T.astype(BF)
        if s:
            GS[s - 1] = picked
            send_list_gate(s).start()
        else:
            EG[0] = picked
    load_wg.wait()
    load_wu.wait()

    def project(c):
        take_x(1, c).wait_recv()
        take_x(2, c).wait_recv()
        load_wd(c).wait()
        x = E[c, 0:3, 0].reshape(3 * cap, cw)
        dy = E[c, 0:3, 1].reshape(3 * cap, cw)
        PRE[...] += dot(x, WGU[pl.ds(pl.multiple_of(c * cw, cw), cw), :])
        BACK[...] += dot(dy, WD[c], 1, 1)

    def forward(c, _):
        for k in range(2):
            load_x(k, c).wait()
            send_y(k, c).wait_recv()
        for k in range(2):
            rows = dot(PICK[...], X[c, k]).astype(BF)
            E[c, 0, k] = rows[0:cap]
            S[c, 0, k] = rows[cap : 2 * cap]
            S[c, 1, k] = rows[2 * cap : 3 * cap]
        send_x(2, c).start()
        send_x(1, c).start()

        @pl.when(c < nc - 2)
        def _():
            cross(c + 2, 0)

        @pl.when(c >= RELAY_LAG)
        def _():
            relays_x(c - RELAY_LAG, pass_x)

        @pl.when(c >= PROJECT_LAG)
        def _():
            project(c - PROJECT_LAG)

        return 0

    lax.fori_loop(0, nc, forward, 0)
    for c in range(nc - RELAY_LAG, nc):
        relays_x(c, pass_x)

    def project_last(c, _):
        project(c)
        return 0

    lax.fori_loop(nc - PROJECT_LAG, nc, project_last, 0)
    send_list_gate(1).wait_recv()
    send_list_gate(2).wait_recv()

    for s in range(3):
        rows = slice(s * cap, (s + 1) * cap)
        gate_col = EG[s].astype(F32)[:, s : s + 1]
        pre_gate = PRE[rows, 0:hid]
        pre_up = PRE[rows, hid : 2 * hid]
        back = BACK[rows, :]
        sig = jax.nn.sigmoid(pre_gate)
        active = pre_gate * sig
        hidden = active * pre_up
        part = jnp.sum(hidden * back, axis=1, keepdims=True)
        part = jnp.broadcast_to(part, (cap, cap)).T[0:8, :]
        if s == 0:
            GG[0, 0] = part
        else:
            GGS[s - 1] = part
        grad = back * gate_col
        HW[rows, :] = (hidden * gate_col).astype(BF)
        PGU[rows, 0:hid] = (grad * pre_up * sig * (1.0 + pre_gate * (1.0 - sig))).astype(BF)
        PGU[rows, hid : 2 * hid] = (grad * active).astype(BF)

    def results(c, _):
        weighted = dot(HW[...], WD[c]).astype(BF)
        in_grad = dot(PGU[...], WGU[pl.ds(pl.multiple_of(c * cw, cw), cw), :], 1, 1).astype(BF)
        for k, value in enumerate((weighted, in_grad)):
            RR[c, 0, k] = value[0:cap]
            R[c, 0, k] = value[cap : 2 * cap]
            R[c, 1, k] = value[2 * cap : 3 * cap]
        send_back(2, c).start()
        send_back(1, c).start()
        return 0

    lax.fori_loop(0, AHEAD, results, 0)
    for s, rel in routes:
        send_gate_grad(s, rel).start()

    def store_w(k, c):
        target = (o_dg, o_du)[k].at[0, pl.ds(pl.multiple_of(c * cw, cw), cw), :]
        return pltpu.make_async_copy(DGU.at[c, :, pl.ds(k * hid, hid)], target, st_w.at[k, c])

    def store_d(c):
        return pltpu.make_async_copy(DD.at[c], o_dd.at[0, :, cols(c)], st_d.at[c])

    def weight_grads(c):
        x = E[c, 0:3, 0].reshape(3 * cap, cw)
        dy = E[c, 0:3, 1].reshape(3 * cap, cw)
        DGU[c] = dot(x, PGU[...], 0, 0).astype(BF)
        DD[c] = dot(HW[...], dy, 0, 0).astype(BF)
        store_w(0, c).start()
        store_w(1, c).start()
        store_d(c).start()

    def store_out(k, c):
        return pltpu.make_async_copy(OUT.at[c, k], (o_mix, o_in)[k].at[:, cols(c)], st_o.at[k, c])

    def finish(c):
        send_sum(c).wait_recv()
        for k in range(2):
            OUT[c, k] = (OWN[c, k] + YR[c, k].astype(F32)).astype(BF)
            store_out(k, c).start()

    def collect(c, _):
        @pl.when(c < nc - AHEAD)
        def _():
            results(c + AHEAD, 0)

        relays_back(c, pass_back)
        take_back(1, c).wait_recv()
        take_back(2, c).wait_recv()
        for k in range(2):
            rows = RR[c, 0:3, k].reshape(3 * cap, cw)
            total = dot(PUT[...], rows)
            YS[c, k] = total[own : 2 * own].astype(BF)
            OWN[c, k] = total[0:own]
        send_sum(c).start()

        weight_grads(c)

        @pl.when(c >= LAG)
        def _():
            finish(c - LAG)

        return 0

    lax.fori_loop(0, nc, collect, 0)

    for s, rel in routes:
        send_gate_grad(s, rel).wait_recv()
    lane = lax.broadcasted_iota(jnp.int32, (own, cap), 1)
    grads = jnp.zeros((own, cap), F32)
    for s in range(3):
        row = GG[s, 0][0:1, :] + GG[s, 1][0:1, :]
        named = PUT[0:own, s * cap : (s + 1) * cap].astype(F32)
        column = jnp.sum(jnp.where(named > 0.5, jnp.broadcast_to(row, (own, cap)), 0.0), axis=1, keepdims=True)
        grads = jnp.where(lane == s, column, grads)
    o_gate[...] = grads.T[0:3, :]

    def finish_last(c, _):
        finish(c)
        return 0

    lax.fori_loop(nc - LAG, nc, finish_last, 0)

    send_gate().wait_send()
    for s in (1, 2):
        send_list_gate(s).wait_send()
    for s, rel in routes:
        send_gate_grad(s, rel).wait_send()

    def drain(c, _):
        for k in range(2):
            send_y(k, c).wait_send()
            store_w(k, c).wait()
            store_out(k, c).wait()
        for s in (1, 2):
            send_x(s, c).wait_send()
            send_back(s, c).wait_send()
        send_sum(c).wait_send()
        store_d(c).wait()
        relays_x(c, lambda s, c: relay_x(s, c).wait_send())
        relays_back(c, lambda s, c: relay_back(s, c).wait_send())
        return 0

    lax.fori_loop(0, nc, drain, 0)


def hand_out(arrays):
    big = [i for i, a in enumerate(arrays) if a.size > 4096]

    def body(*refs):
        n = len(arrays)
        src, dst = refs[:n], refs[n : 2 * n]
        wr = refs[-1]
        copies = [pltpu.make_async_copy(src[i], dst[i], wr.at[j]) for j, i in enumerate(big)]
        for copy in copies:
            copy.start()
        for i in range(n):
            if i not in big:
                dst[i][...] = src[i][...]
        for copy in copies:
            copy.wait()

    specs = [pl.BlockSpec(memory_space=pl.ANY if i in big else pltpu.VMEM) for i in range(len(arrays))]
    return pl.pallas_call(
        body,
        out_shape=tuple(jax.ShapeDtypeStruct(a.shape, a.dtype) for a in arrays),
        in_specs=specs,
        out_specs=tuple(specs),
        scratch_shapes=[pltpu.SemaphoreType.DMA((len(big),))],
        compiler_params=pltpu.CompilerParams(vmem_limit_bytes=1024 * 1024),
        name="hand_out",
    )(*arrays)


def on_device(tokens, cotangent, gate_probs, slot_rows, w_gate, w_up, w_down):
    own, width = tokens.shape
    cycle, cap = slot_rows.shape
    hid = w_gate.shape[2]
    nc, cw = CHUNKS, width // CHUNKS
    group, lists = 2 * own, cycle * cap
    blocks = lax.axis_size("blk")
    hops = 2 * (cycle - 1)
    dma = pltpu.SemaphoreType.DMA
    vmem = pltpu.VMEM
    any_space = pl.BlockSpec(memory_space=pl.ANY)
    in_vmem = pl.BlockSpec(memory_space=pltpu.VMEM)

    def hold(a):
        return pltpu.with_memory_space_constraint(a, pltpu.HBM)

    def body(*refs):
        kernel(blocks, *refs)

    outs = pl.pallas_call(
        body,
        out_shape=(
            jax.ShapeDtypeStruct((own, width), BF),
            jax.ShapeDtypeStruct((own, width), BF),
            jax.ShapeDtypeStruct((cycle, own), F32),
            jax.ShapeDtypeStruct(w_gate.shape, BF),
            jax.ShapeDtypeStruct(w_up.shape, BF),
            jax.ShapeDtypeStruct(w_down.shape, BF),
        ),
        in_specs=[any_space, any_space, any_space, in_vmem, any_space, any_space, any_space],
        out_specs=(any_space, any_space, in_vmem, any_space, any_space, any_space),
        scratch_shapes=[
            vmem((nc, 2, group, cw), BF),
            vmem((nc, 1 + hops, 2, cap, cw), BF),
            vmem((nc, cycle - 1, 2, cap, cw), BF),
            vmem((2, cycle, own), BF),
            vmem((cycle, cap, cap), BF),
            vmem((cycle - 1, cap, cap), BF),
            vmem((width, 2 * hid), BF),
            vmem((nc, hid, cw), BF),
            vmem((lists, group), BF),
            vmem((group, lists), BF),
            vmem((lists, 2 * hid), F32),
            vmem((lists, hid), F32),
            vmem((lists, 2 * hid), BF),
            vmem((lists, hid), BF),
            vmem((nc, cycle - 1, 2, cap, cw), BF),
            vmem((nc, 1 + hops, 2, cap, cw), BF),
            vmem((cycle, 2, 8, cap), F32),
            vmem((cycle - 1, 8, cap), F32),
            vmem((nc, 2, own, cw), F32),
            vmem((nc, 2, own, cw), BF),
            vmem((nc, 2, own, cw), BF),
            vmem((nc, 2, own, cw), BF),
            vmem((nc, cw, 2 * hid), BF),
            vmem((nc, hid, cw), BF),
            dma((2, nc)), dma((2,)), dma((nc,)), dma,
            dma((2, nc)), dma((2, nc)), dma, dma,
            dma((hops, nc)), dma((hops, nc)), dma((2,)), dma((2,)),
            dma((hops, nc)), dma((hops, nc)), dma((cycle, 2)), dma((cycle, 2)),
            dma((nc,)), dma((nc,)),
            dma((2, nc)), dma((2, nc)), dma((nc,)),
        ],
        compiler_params=pltpu.CompilerParams(
            collective_id=0, has_side_effects=True, vmem_limit_bytes=46 * 1024 * 1024
        ),
        name="routed_experts",
    )(hold(tokens), hold(cotangent), hold(gate_probs.T), slot_rows, hold(w_gate), hold(w_up), hold(w_down))
    mixed, in_grad, gates, d_gate, d_up, d_down = hand_out(outs)
    return mixed, in_grad, gates.T, d_gate, d_up, d_down


def solution(mesh):
    in_specs = (
        P(("blk", "dp"), None),
        P(("blk", "dp"), None),
        P(("blk", "dp"), None),
        P("blk", None),
        P("blk", None, "dp"),
        P("blk", None, "dp"),
        P("blk", "dp", None),
    )
    out_specs = (
        P(("blk", "dp"), None),
        P(("blk", "dp"), None),
        P(("blk", "dp"), None),
        P("blk", None, "dp"),
        P("blk", None, "dp"),
        P("blk", "dp", None),
    )
    return jax.shard_map(
        on_device, mesh=mesh, in_specs=in_specs, out_specs=out_specs, check_vma=False
    )
```
